32 devices in a mesh: leaf: 4 (over y, x), col: 8 (over z, core).
Axes of the slice: x: 2, y: 2, z: 4, core: 2. Of those that a mesh axis runs over, the one named last changes fastest.
Arguments:
- s_blocks: bfloat16 [64, 8, 128, 128], P(('leaf', 'col')), may hold values from -0.0059814453 to 0.0059814453
- z_blocks: bfloat16 [64, 8, 128, 128], P(('leaf', 'col')), may hold values from -1.5 to 1.5
- s_requests: int32 [4, 8, 8, 1], P('leaf', 'col'), may hold values from -1 to 15, as said below
- y_pairs: int32 [64, 8, 8], P(('leaf', 'col')), may hold values from -1 to 7, as said below
- zt_requests: int32 [4, 8, 8, 1], P('leaf', 'col'), may hold values from -1 to 31, as said below
- d_pairs: int32 [64, 8, 8], P(('leaf', 'col')), may hold values from -1 to 7, as said below
- d_requests: int32 [4, 8, 8, 1], P('leaf', 'col'), may hold values from -1 to 31, as said below
- e_pairs: int32 [64, 8, 8], P(('leaf', 'col')), may hold values from -1 to 7, as said below
- z_requests: int32 [4, 8, 8, 1], P('leaf', 'col'), may hold values from -1 to 31, as said below
- z_pairs: int32 [64, 8, 8], P(('leaf', 'col')), may hold values from -1 to 7, as said below
Outputs:
- z_refined: bfloat16 [64, 8, 128, 128], P(('leaf', 'col'))
The draws below stay inside these ranges and needn't reach their ends.
Inputs may be any that keep to these rules, and one draw needn't show every extreme that they name: `s_requests`: entry [l, c, p, q] is -1 or a slot of the S holdings of the device (l, p); the entries of one [l, c, p] are distinct. Every reader has some peer with all 1 entries used, and one reader uses all entries. `zt_requests`: entry [l, c, p, q] is -1 or a slot of the Z holdings of the device (l, p); the entries of one [l, c, p] are distinct. Every reader has some peer with all 1 entries used, and one reader uses all entries. `d_requests`: entry [l, c, p, q] is -1 or a slot of the D holdings of the device (l, p); the entries of one [l, c, p] are distinct. Every reader has some peer with all 1 entries used, and one reader uses all entries. `z_requests`: entry [l, c, p, q] is -1 or a slot of the Z holdings of the device (l, p); the entries of one [l, c, p] are distinct. Every reader has some peer with all 1 entries used, and one reader uses all entries. `y_pairs`: each entry is -1 or the position p + q of an entry of s_requests that is not -1, for the reader holding the column; every such entry is named at least once. `d_pairs`: each entry is -1 or the position p + q of an entry of zt_requests that is not -1, for the reader holding the column; every such entry is named at least once. `e_pairs`: each entry is -1 or the position p + q of an entry of d_requests that is not -1, for the reader holding the column; every such entry is named at least once. `z_pairs`: each entry is -1 or the position p + q of an entry of z_requests that is not -1, for the reader holding the column; every such entry is named at least once.
All inputs are finite; a program needn't handle non-finite values.
Results may differ from the reference program's by a relative error of at most 0.0059.
Values may be sent and summed in bfloat16 or wider, within the bound.
A program may use at most 64 MiB of HBM per device.

```python
import jax
import jax.numpy as jnp
from jax import lax

BLOCK = 128
SLOTS = 8
CAP = 1
CD = 2
NBC = 64
N_LEAF = 4
N_COL = 8


def request_lists(key, hold_count):
    readers = N_LEAF * N_COL
    fetch_total = N_COL * CAP
    triples = CD * SLOTS * SLOTS
    subkeys = jax.random.split(key, 7)
    reader_load = jax.random.randint(subkeys[0], (readers, 1), 1, 4)
    counts = jnp.minimum(jax.random.randint(subkeys[1], (readers, N_COL), 0, 12) % (reader_load + 1), CAP)
    busy_peer = jax.random.randint(subkeys[2], (readers, 1), 0, N_COL)
    full_reader = jax.random.randint(subkeys[3], (), 0, readers)
    peer_ids = jnp.arange(N_COL)[None, :]
    reader_ids = jnp.arange(readers)[:, None]
    counts = jnp.where((peer_ids == busy_peer) | (reader_ids == full_reader), CAP, counts)
    scores = jax.random.randint(subkeys[4], (readers, N_COL, hold_count), 0, 1 << 20) * hold_count + jnp.arange(hold_count)
    ranked = jnp.argsort(scores, axis=-1)[:, :, :CAP]
    asked_ids = jnp.where(jnp.arange(CAP)[None, None, :] < counts[:, :, None], ranked, -1).astype(jnp.int32)
    live_mask = (asked_ids >= 0).reshape(readers, fetch_total)
    slot_scores = jax.random.randint(subkeys[5], (readers, triples), 0, 1 << 20) * triples + jnp.arange(triples)
    slot_order = jnp.argsort(slot_scores, axis=-1)
    position = jnp.broadcast_to(jnp.arange(triples)[None, :], (readers, triples))
    spare_ids = jax.random.randint(subkeys[6], (readers, triples), 0, fetch_total)
    wanted = jnp.where(position < fetch_total, position, spare_ids)
    wanted_live = jnp.take_along_axis(live_mask, wanted, axis=-1)
    entries = jnp.where(wanted_live, wanted, -1)
    inverse = jnp.argsort(slot_order, axis=-1)
    pair_ids = jnp.take_along_axis(entries, inverse, axis=-1).astype(jnp.int32)
    return (asked_ids.reshape(N_LEAF, N_COL, N_COL, CAP), pair_ids.reshape(NBC, SLOTS, SLOTS))


def draw_s_requests(key, part):
    return request_lists(jax.random.fold_in(key, 11), CD * SLOTS)[0]


def draw_y_pairs(key, part):
    return request_lists(jax.random.fold_in(key, 11), CD * SLOTS)[1]


def draw_zt_requests(key, part):
    return request_lists(jax.random.fold_in(key, 12), 2 * CD * SLOTS)[0]


def draw_d_pairs(key, part):
    return request_lists(jax.random.fold_in(key, 12), 2 * CD * SLOTS)[1]


def draw_d_requests(key, part):
    return request_lists(jax.random.fold_in(key, 13), 2 * CD * SLOTS)[0]


def draw_e_pairs(key, part):
    return request_lists(jax.random.fold_in(key, 13), 2 * CD * SLOTS)[1]


def draw_z_requests(key, part):
    return request_lists(jax.random.fold_in(key, 14), 2 * CD * SLOTS)[0]


def draw_z_pairs(key, part):
    return request_lists(jax.random.fold_in(key, 14), 2 * CD * SLOTS)[1]


def block_levels(stream_key, dims, cuts, smallest, high):
    def one(dim, parts):
        draws = jax.random.uniform(jax.random.fold_in(jax.random.fold_in(stream_key, 6), dim), (parts,), jnp.float32, smallest / len(cuts), high / len(cuts))
        return jnp.repeat(jnp.exp(draws), dims[dim] // parts).reshape((-1,) + (1,) * (len(dims) - dim - 1))

    gain = one(*cuts[0])
    for cut in cuts[1:]:
        gain = gain * one(*cut)
    return gain


def gaussian(stream_key, extent, spread, bound, shards=(), kind=jnp.bfloat16):
    array = spread * jax.random.normal(stream_key, extent, jnp.float32)
    if shards:
        array = array * block_levels(stream_key, extent, shards, -0.22, 0.18)
    return jnp.clip(array, -bound, bound).astype(kind)


def setup_inputs(seed: int = 0) -> dict:
    key_list = jax.random.split(jax.random.key(seed), 11)
    return {
        "s_blocks": gaussian(key_list[0], (NBC, SLOTS, BLOCK, BLOCK), 0.001, 0.0059814453, ((0, 32),)),
        "z_blocks": gaussian(key_list[1], (NBC, SLOTS, BLOCK, BLOCK), 0.25, 1.5, ((0, 32),)),
        "s_requests": draw_s_requests(jax.random.fold_in(key_list[10], 71), 0),
        "y_pairs": draw_y_pairs(jax.random.fold_in(key_list[10], 71), 0),
        "zt_requests": draw_zt_requests(jax.random.fold_in(key_list[10], 71), 0),
        "d_pairs": draw_d_pairs(jax.random.fold_in(key_list[10], 71), 0),
        "d_requests": draw_d_requests(jax.random.fold_in(key_list[10], 71), 0),
        "e_pairs": draw_e_pairs(jax.random.fold_in(key_list[10], 71), 0),
        "z_requests": draw_z_requests(jax.random.fold_in(key_list[10], 71), 0),
        "z_pairs": draw_z_pairs(jax.random.fold_in(key_list[10], 71), 0),
    }


def holdings_of(blocks):
    return blocks.reshape(N_LEAF, N_COL, CD * SLOTS, BLOCK, BLOCK)


def fetch_for(own_blocks, requests, reader):
    hold_count = own_blocks.shape[2]
    leaf_index = reader // N_COL
    partner = leaf_index + 1 - 2 * (leaf_index % 2)
    from_partner = requests >= hold_count
    source_leaf = jnp.where(from_partner, partner, leaf_index).astype(jnp.int32)
    source_slot = jnp.maximum(jnp.where(from_partner, requests - hold_count, requests), 0).astype(jnp.int32)
    peer_ids = jnp.broadcast_to(jnp.arange(N_COL, dtype=jnp.int32)[:, None], requests.shape)
    blocks = own_blocks[source_leaf, peer_ids, source_slot]
    blocks = jnp.where((requests >= 0)[:, :, None, None], blocks, jnp.zeros_like(blocks))
    return blocks.reshape(N_COL * CAP, BLOCK, BLOCK)


def block_products(fetched, pair_ids, local_blocks, flipped):
    fetch_count = fetched.shape[0]
    padded = jnp.concatenate([fetched, jnp.zeros((1,) + fetched.shape[1:], fetched.dtype)], axis=0)
    lookup = jnp.where(pair_ids < 0, fetch_count, pair_ids).astype(jnp.int32)
    chosen = jnp.take(padded, lookup, axis=0).astype(jnp.float32)
    einsum_form = "gabji,gbjk->gaik" if flipped else "gabij,gbjk->gaik"
    return jnp.einsum(einsum_form, chosen, local_blocks.astype(jnp.float32))


def product_pass(own_blocks, requests, pair_ids, local_blocks, flipped):
    readers = N_LEAF * N_COL
    asked_ids = requests.reshape(readers, N_COL, CAP)
    paired = pair_ids.reshape(readers, CD, SLOTS, SLOTS)
    local_rows = local_blocks.reshape(readers, CD, SLOTS, BLOCK, BLOCK)

    def one_reader(packed):
        reader, reader_asks, reader_pairs, reader_local = packed
        fetched = fetch_for(own_blocks, reader_asks, reader)
        return block_products(fetched, reader_pairs, reader_local, flipped)

    result = lax.map(one_reader, (jnp.arange(readers, dtype=jnp.int32), asked_ids, paired, local_rows))
    return result.reshape(NBC, SLOTS, BLOCK, BLOCK)


def reference(s_blocks, z_blocks, s_requests, y_pairs, zt_requests, d_pairs, d_requests, e_pairs, z_requests, z_pairs):
    s_own = holdings_of(s_blocks)
    z_own = holdings_of(z_blocks)
    y_blocks = product_pass(s_own, s_requests, y_pairs, z_blocks, False).astype(jnp.bfloat16)
    first_slot = (jnp.arange(SLOTS) == 0).astype(jnp.float32)
    identity = first_slot[:, None, None] * jnp.eye(BLOCK, dtype=jnp.float32)
    d_blocks = (identity - product_pass(z_own, zt_requests, d_pairs, y_blocks, True)).astype(jnp.bfloat16)
    square = product_pass(holdings_of(d_blocks), d_requests, e_pairs, d_blocks, False)
    e_blocks = (0.5 * d_blocks.astype(jnp.float32) + 0.375 * square).astype(jnp.bfloat16)
    refined = z_blocks.astype(jnp.float32) + product_pass(z_own, z_requests, z_pairs, e_blocks, False)
    return refined.astype(jnp.bfloat16)
```

```python
import functools

import jax
import jax.numpy as jnp
from jax import lax
from jax.experimental import pallas as pl
from jax.experimental.pallas import tpu as pltpu
from jax.sharding import PartitionSpec as P

MESH = pl.DeviceIdType.MESH
S, T, Z, D = range(4)
OWN, OTHER = range(2)


def kernel(
    n,
    per,
    cap,
    cols,
    slots,
    s_asks,
    t_asks,
    z_asks,
    d_asks,
    y_names,
    d_names,
    e_names,
    z_names,
    s_hbm,
    z_hbm,
    out_ref,
    req_ref,
    allreq,
    y_pairs,
    d_pairs,
    e_pairs,
    z_pairs,
    s_ref,
    z_ref,
    send_s,
    send_t,
    send_z,
    send_d,
    xs_t,
    xs_z,
    xs_d,
    xr_t,
    xr_z,
    xr_d,
    f_s,
    f_t,
    f_z,
    f_d,
    y_ref,
    d_ref,
    e_ref,
    go_sem,
    req_send,
    req_recv,
    in_sem,
    z_send,
    z_recv,
    x_send,
    x_recv,
):
    leaf = lax.axis_index("leaf")
    me = lax.axis_index("col")
    odd = lax.rem(leaf, 2)
    partner = leaf + 1 - 2 * odd
    chips = n // per
    chip = lax.div(me, per)
    hold = cols * slots
    size = z_ref.shape[1]
    fetch = n * cap
    pairs = {S: y_pairs, T: d_pairs, D: e_pairs, Z: z_pairs}
    asks = (s_asks, t_asks, z_asks, d_asks)
    moves = [(a, req_ref.at[pl.ds(kind, 1)]) for kind, a in enumerate(asks)]
    moves += [(s_hbm, s_ref), (z_hbm, z_ref)]
    moves += [(y_names, y_pairs), (d_names, d_pairs), (e_names, e_pairs), (z_names, z_pairs)]
    loads = [pltpu.make_async_copy(a, b, in_sem.at[i]) for i, (a, b) in enumerate(moves)]
    sends = {S: send_s, T: send_t, Z: send_z, D: send_d}
    fetched = {S: f_s, T: f_t, Z: f_z, D: f_d}
    xsends = {T: xs_t, Z: xs_z, D: xs_d}
    xrecvs = {T: xr_t, Z: xr_z, D: xr_d}
    leaves = (leaf, partner)

    def span(low, high, body):
        def step(k, carry):
            body(k)
            return carry

        lax.fori_loop(low, high, step, 0)

    def each_chip(low, high, body):
        def step(k, carry):
            body(k)
            return carry

        lax.fori_loop(low, high, step, 0, unroll=n <= 8)

    barrier = pltpu.get_barrier_semaphore()

    def greet(to_leaf, to):
        pl.semaphore_signal(barrier, inc=1, device_id=(to_leaf, to), device_id_type=MESH)

    def greet_chip(side, c):
        for i in range(per):
            greet(leaves[side], c * per + i)

    def tell_chip(side, c):
        for i in range(per):
            pl.semaphore_signal(
                go_sem.at[side, chip],
                inc=1,
                device_id=(leaves[side], c * per + i),
                device_id_type=MESH,
            )

    for i in range(1, per):
        greet(leaf, chip * per + lax.rem(me + i, per))
    for load in loads:
        load.start()

    @pl.when(odd == 0)
    def _():
        greet_chip(OTHER, chip)

    def greet_up(c):
        greet_chip(OWN, c)
        greet_chip(OTHER, c)

    span(chip + 1, chips, greet_up)
    for f in (f_s, f_t, f_z, f_d):
        f[fetch] = jnp.zeros((size, size), f.dtype)
    pl.semaphore_wait(barrier, per - 1 + per * odd + 2 * per * chip)

    @pl.when(odd == 1)
    def _():
        tell_chip(OTHER, chip)

    def tell_down(k):
        tell_chip(OWN, chip - k)
        tell_chip(OTHER, chip - k)

    span(1, chip + 1, tell_down)
    for load in loads[:4]:
        load.wait()
    own_copy = pltpu.make_async_copy(req_ref, allreq.at[me], req_recv.at[OWN, chip])
    own_copy.start()

    def req_copy(side, to):
        return pltpu.make_async_remote_copy(
            src_ref=req_ref,
            dst_ref=allreq.at[side * n + me],
            send_sem=req_send.at[side],
            recv_sem=req_recv.at[side, chip],
            device_id=(leaves[side], to),
            device_id_type=MESH,
        )

    def ask_chip(side, c):
        for i in range(per):
            req_copy(side, c * per + i).start()

    for i in range(1, per):
        req_copy(OWN, chip * per + lax.rem(me + i, per)).start()

    @pl.when(odd == 1)
    def _():
        ask_chip(OTHER, chip)

    def ask_down(k):
        ask_chip(OWN, chip - k)
        ask_chip(OTHER, chip - k)

    span(1, chip + 1, ask_down)

    @pl.when(odd == 0)
    def _():
        pl.semaphore_wait(go_sem.at[OTHER, chip], per)
        ask_chip(OTHER, chip)

    def ask_up(c):
        for side in (OWN, OTHER):
            pl.semaphore_wait(go_sem.at[side, c], per)
            ask_chip(side, c)

    span(chip + 1, chips, ask_up)
    for load in loads[4:6]:
        load.wait()

    def asked(side, c):
        rows = allreq.at[pl.ds(side * n + c * per, per)]
        pltpu.make_async_remote_copy(
            src_ref=rows,
            dst_ref=rows,
            send_sem=req_send.at[side],
            recv_sem=req_recv.at[side, c],
            device_id=(leaf, me),
            device_id_type=MESH,
        ).wait_recv()

    def ask(kind, side, c, q):
        return allreq[side * n + c, kind, me * cap + q]

    def x_copy(kind, first, count, group):
        part = pl.ds(first * cap, count * cap)
        return pltpu.make_async_remote_copy(
            src_ref=xsends[kind].at[part],
            dst_ref=xrecvs[kind].at[part],
            send_sem=x_send.at[kind],
            recv_sem=x_recv.at[kind, group],
            device_id=(partner, me),
            device_id_type=MESH,
        )

    def z_copy(kind, to):
        return pltpu.make_async_remote_copy(
            src_ref=sends[kind].at[pl.ds(to * cap, cap)],
            dst_ref=fetched[kind].at[pl.ds(me * cap, cap)],
            send_sem=z_send.at[kind],
            recv_sem=z_recv.at[kind],
            device_id=(leaf, to),
            device_id_type=MESH,
        )

    def z_all(kind):
        part = pl.ds(0, (n - 1) * cap)
        return pltpu.make_async_remote_copy(
            src_ref=sends[kind].at[part],
            dst_ref=fetched[kind].at[part],
            send_sem=z_send.at[kind],
            recv_sem=z_recv.at[kind],
            device_id=(leaf, me),
            device_id_type=MESH,
        )

    def x_chip(kind, own_ref, g):
        for i in range(per):
            c = g * per + i
            for q in range(cap):
                slot = jnp.clip(ask(kind, OTHER, c, q) - hold, 0, hold - 1)
                xsends[kind][c * cap + q] = own_ref[slot]
            x_copy(kind, c, 1, g).start()

    def z_chip(kind, own_ref, g):
        if kind != S:
            x_copy(kind, g * per, per, g).wait_recv()
        for i in range(per):
            c = g * per + i
            for q in range(cap):
                request = ask(kind, OWN, c, q)
                block = own_ref[jnp.clip(request, 0, hold - 1)]
                if kind != S:
                    block = jnp.where(request < hold, block, xrecvs[kind][c * cap + q])
                if kind == T:
                    block = block.T
                sends[kind][c * cap + q] = block

            @pl.when(c != me)
            def _(c=c):
                z_copy(kind, c).start()

    def keep(kind):
        for q in range(cap):
            fetched[kind][me * cap + q] = sends[kind][me * cap + q]

    def near(j):
        below = lax.div(chip + chips - j, chips)
        return j + below * (chip - 2 * j)

    def arrived(kind):
        z_all(kind).wait_recv()

    def product(kind, local_ref, finish):
        f = fetched[kind]

        def body(g):
            rhs = local_ref[pl.ds(g * slots, slots)].reshape(slots * size, size)
            for a in range(slots):
                blocks = []
                for b in range(slots):
                    name = pairs[kind][g, a, b]
                    blocks.append(f[jnp.where(name < 0, fetch, name)])
                lhs = jnp.concatenate(blocks, axis=1)
                finish(g * slots + a, a, jnp.dot(lhs, rhs, preferred_element_type=jnp.float32))

        lax.fori_loop(0, cols, lambda g, c: (body(g), c)[1], 0, unroll=True)

    def first(j):
        g = near(j)
        asked(OWN, g)
        z_chip(S, s_ref, g)
        asked(OTHER, g)
        x_chip(T, z_ref, g)

    with jax.named_scope("first"):
        each_chip(0, chips, first)
    with jax.named_scope("xZ"):
        each_chip(0, chips, lambda g: x_chip(Z, z_ref, g))
    with jax.named_scope("zT"):
        each_chip(0, chips, lambda j: z_chip(T, z_ref, near(j)))
        keep(S)
        keep(T)

    for load in loads[6:]:
        load.wait()
    with jax.named_scope("arrS"):
        arrived(S)

    def y_finish(i, a, total):
        y_ref[i] = total.astype(y_ref.dtype)

    with jax.named_scope("pY"):
        product(S, z_ref, y_finish)
    half = (chips + 1) // 2
    with jax.named_scope("zZ1"):
        each_chip(0, half, lambda g: z_chip(Z, z_ref, g))
    with jax.named_scope("arrT"):
        arrived(T)

    def d_finish(i, a, total):
        rows = lax.broadcasted_iota(jnp.int32, (size, size), 0)
        columns = lax.broadcasted_iota(jnp.int32, (size, size), 1)
        one = 1.0 if a == 0 else 0.0
        d_ref[i] = (jnp.where(rows == columns, one, 0.0) - total).astype(d_ref.dtype)

    with jax.named_scope("pD"):
        product(T, y_ref, d_finish)
    with jax.named_scope("xD"):
        each_chip(0, chips, lambda g: x_chip(D, d_ref, g))
    with jax.named_scope("zZ2"):
        each_chip(half, chips, lambda g: z_chip(Z, z_ref, g))
        keep(Z)
    with jax.named_scope("zD"):
        each_chip(0, chips, lambda g: z_chip(D, d_ref, g))
        keep(D)
    with jax.named_scope("arrD"):
        arrived(D)

    def e_finish(i, a, total):
        e_ref[i] = (0.5 * d_ref[i].astype(jnp.float32) + 0.375 * total).astype(e_ref.dtype)

    with jax.named_scope("pE"):
        product(D, d_ref, e_finish)
    with jax.named_scope("arrZ"):
        arrived(Z)

    def z_finish(i, a, total):
        out_ref[i] = (z_ref[i].astype(jnp.float32) + total).astype(out_ref.dtype)

    with jax.named_scope("pO"):
        product(Z, e_ref, z_finish)

    for side in (OWN, OTHER):
        rows = allreq.at[pl.ds(0, n - 1 + side)]
        pltpu.make_async_remote_copy(
            src_ref=rows,
            dst_ref=rows,
            send_sem=req_send.at[side],
            recv_sem=req_recv.at[side, 0],
            device_id=(leaf, me),
            device_id_type=MESH,
        ).wait_send()
    for kind in (S, T, Z, D):
        z_all(kind).wait_send()
        if kind != S:
            x_copy(kind, 0, n, 0).wait_send()


def on_device(
    n,
    s_blocks,
    z_blocks,
    s_requests,
    y_pairs,
    zt_requests,
    d_pairs,
    d_requests,
    e_pairs,
    z_requests,
    z_pairs,
):
    cols, slots, size = z_blocks.shape[:3]
    cap = s_requests.shape[3]
    per = 1 + (n + 1) % 2
    hold = cols * slots
    flat = (hold, size, size)
    fetch = n * cap
    asks = [
        r.reshape(1, fetch) for r in (s_requests, zt_requests, z_requests, d_requests)
    ]
    names = [y_pairs, d_pairs, e_pairs, z_pairs]
    kind = z_blocks.dtype

    def blocks(count):
        return pltpu.VMEM((count, size, size), kind)

    hbm = pl.BlockSpec(memory_space=pltpu.HBM)
    refined = pl.pallas_call(
        functools.partial(kernel, n, per, cap, cols, slots),
        out_shape=pltpu.VMEM(flat, kind),
        in_specs=[hbm] * 10,
        out_specs=pl.BlockSpec(memory_space=pltpu.VMEM),
        scratch_shapes=[
            pltpu.SMEM((4, fetch), jnp.int32),
            pltpu.SMEM((2 * n, 4, fetch), jnp.int32),
        ]
        + [pltpu.SMEM(y_pairs.shape, jnp.int32) for _ in range(4)]
        + [blocks(hold) for _ in range(2)]
        + [blocks(fetch) for _ in range(10)]
        + [blocks(fetch + 1) for _ in range(4)]
        + [blocks(hold) for _ in range(3)]
        + [
            pltpu.SemaphoreType.REGULAR((2, n // per)),
            pltpu.SemaphoreType.DMA((2,)),
            pltpu.SemaphoreType.DMA((2, n // per)),
            pltpu.SemaphoreType.DMA((10,)),
            pltpu.SemaphoreType.DMA((4,)),
            pltpu.SemaphoreType.DMA((4,)),
            pltpu.SemaphoreType.DMA((4,)),
            pltpu.SemaphoreType.DMA((4, n // per)),
        ],
        compiler_params=pltpu.CompilerParams(
            collective_id=0, has_side_effects=True, vmem_limit_bytes=66326528
        ),
    )(*asks, *names, s_blocks.reshape(flat), z_blocks.reshape(flat))
    return refined.reshape(z_blocks.shape)


def solution(mesh):
    flat4 = P(("leaf", "col"), None, None, None)
    flat3 = P(("leaf", "col"), None, None)
    asks = P("leaf", "col", None, None)
    in_specs = (flat4, flat4, asks, flat3, asks, flat3, asks, flat3, asks, flat3)
    return jax.shard_map(
        functools.partial(on_device, mesh.shape["col"]),
        mesh=mesh,
        in_specs=in_specs,
        out_specs=flat4,
        check_vma=False,
    )
```

```python
import functools

import jax
import jax.numpy as jnp
from jax import lax
from jax.experimental import pallas as pl
from jax.experimental.pallas import tpu as pltpu
from jax.sharding import PartitionSpec as P

MESH = pl.DeviceIdType.MESH
S, T, Z, D = range(4)
OWN, OTHER = range(2)


def kernel(
    n,
    per,
    cap,
    cols,
    slots,
    s_asks,
    t_asks,
    z_asks,
    d_asks,
    y_names,
    d_names,
    e_names,
    z_names,
    s_hbm,
    z_hbm,
    out_ref,
    req_ref,
    allreq,
    y_pairs,
    d_pairs,
    e_pairs,
    z_pairs,
    s_ref,
    z_ref,
    send_s,
    send_t,
    send_z,
    send_d,
    xs_t,
    xs_z,
    xs_d,
    xr_t,
    xr_z,
    xr_d,
    f_s,
    f_t,
    f_z,
    f_d,
    y_ref,
    d_ref,
    e_ref,
    go_sem,
    req_send,
    req_recv,
    in_sem,
    z_send,
    z_recv,
    x_send,
    x_recv,
):
    leaf = lax.axis_index("leaf")
    me = lax.axis_index("col")
    odd = lax.rem(leaf, 2)
    partner = leaf + 1 - 2 * odd
    chips = n // per
    chip = lax.div(me, per)
    hold = cols * slots
    size = z_ref.shape[1]
    fetch = n * cap
    pairs = {S: y_pairs, T: d_pairs, D: e_pairs, Z: z_pairs}
    asks = (s_asks, t_asks, z_asks, d_asks)
    moves = [(a, req_ref.at[pl.ds(kind, 1)]) for kind, a in enumerate(asks)]
    moves += [(s_hbm, s_ref), (z_hbm, z_ref)]
    moves += [(y_names, y_pairs), (d_names, d_pairs), (e_names, e_pairs), (z_names, z_pairs)]
    loads = [pltpu.make_async_copy(a, b, in_sem.at[i]) for i, (a, b) in enumerate(moves)]
    sends = {S: send_s, T: send_t, Z: send_z, D: send_d}
    fetched = {S: f_s, T: f_t, Z: f_z, D: f_d}
    xsends = {T: xs_t, Z: xs_z, D: xs_d}
    xrecvs = {T: xr_t, Z: xr_z, D: xr_d}
    leaves = (leaf, partner)

    def span(low, high, body):
        def step(k, carry):
            body(k)
            return carry

        lax.fori_loop(low, high, step, 0)

    def each_chip(low, high, body):
        def step(k, carry):
            body(k)
            return carry

        lax.fori_loop(low, high, step, 0, unroll=n <= 8)

    barrier = pltpu.get_barrier_semaphore()

    def greet(to_leaf, to):
        pl.semaphore_signal(barrier, inc=1, device_id=(to_leaf, to), device_id_type=MESH)

    def greet_chip(side, c):
        for i in range(per):
            greet(leaves[side], c * per + i)

    def tell_chip(side, c):
        for i in range(per):
            pl.semaphore_signal(
                go_sem.at[side, chip],
                inc=1,
                device_id=(leaves[side], c * per + i),
                device_id_type=MESH,
            )

    for i in range(1, per):
        greet(leaf, chip * per + lax.rem(me + i, per))
    for load in loads:
        load.start()

    @pl.when(odd == 0)
    def _():
        greet_chip(OTHER, chip)

    def greet_up(c):
        greet_chip(OWN, c)
        greet_chip(OTHER, c)

    span(chip + 1, chips, greet_up)
    for f in (f_s, f_t, f_z, f_d):
        f[fetch] = jnp.zeros((size, size), f.dtype)
    pl.semaphore_wait(barrier, per - 1 + per * odd + 2 * per * chip)

    @pl.when(odd == 1)
    def _():
        tell_chip(OTHER, chip)

    def tell_down(k):
        tell_chip(OWN, chip - k)
        tell_chip(OTHER, chip - k)

    span(1, chip + 1, tell_down)
    for load in loads[:4]:
        load.wait()
    own_copy = pltpu.make_async_copy(req_ref, allreq.at[me], req_recv.at[OWN, chip])
    own_copy.start()

    def req_copy(side, to):
        return pltpu.make_async_remote_copy(
            src_ref=req_ref,
            dst_ref=allreq.at[side * n + me],
            send_sem=req_send.at[side],
            recv_sem=req_recv.at[side, chip],
            device_id=(leaves[side], to),
            device_id_type=MESH,
        )

    def ask_chip(side, c):
        for i in range(per):
            req_copy(side, c * per + i).start()

    for i in range(1, per):
        req_copy(OWN, chip * per + lax.rem(me + i, per)).start()

    @pl.when(odd == 1)
    def _():
        ask_chip(OTHER, chip)

    def ask_down(k):
        ask_chip(OWN, chip - k)
        ask_chip(OTHER, chip - k)

    span(1, chip + 1, ask_down)

    @pl.when(odd == 0)
    def _():
        pl.semaphore_wait(go_sem.at[OTHER, chip], per)
        ask_chip(OTHER, chip)

    def ask_up(c):
        for side in (OWN, OTHER):
            pl.semaphore_wait(go_sem.at[side, c], per)
            ask_chip(side, c)

    span(chip + 1, chips, ask_up)
    for load in loads[4:6]:
        load.wait()

    def asked(side, c):
        rows = allreq.at[pl.ds(side * n + c * per, per)]
        pltpu.make_async_remote_copy(
            src_ref=rows,
            dst_ref=rows,
            send_sem=req_send.at[side],
            recv_sem=req_recv.at[side, c],
            device_id=(leaf, me),
            device_id_type=MESH,
        ).wait_recv()

    def ask(kind, side, c, q):
        return allreq[side * n + c, kind, me * cap + q]

    def x_copy(kind, first, count, group):
        part = pl.ds(first * cap, count * cap)
        return pltpu.make_async_remote_copy(
            src_ref=xsends[kind].at[part],
            dst_ref=xrecvs[kind].at[part],
            send_sem=x_send.at[kind - 1],
            recv_sem=x_recv.at[kind - 1, group],
            device_id=(partner, me),
            device_id_type=MESH,
        )

    def z_copy(kind, to):
        return pltpu.make_async_remote_copy(
            src_ref=sends[kind].at[pl.ds(to * cap, cap)],
            dst_ref=fetched[kind].at[pl.ds(me * cap, cap)],
            send_sem=z_send.at[kind],
            recv_sem=z_recv.at[kind],
            device_id=(leaf, to),
            device_id_type=MESH,
        )

    def z_all(kind):
        part = pl.ds(0, (n - 1) * cap)
        return pltpu.make_async_remote_copy(
            src_ref=sends[kind].at[part],
            dst_ref=fetched[kind].at[part],
            send_sem=z_send.at[kind],
            recv_sem=z_recv.at[kind],
            device_id=(leaf, me),
            device_id_type=MESH,
        )

    def x_chip(kind, own_ref, g):
        for i in range(per):
            c = g * per + i
            for q in range(cap):
                slot = jnp.clip(ask(kind, OTHER, c, q) - hold, 0, hold - 1)
                xsends[kind][c * cap + q] = own_ref[slot]
            x_copy(kind, c, 1, g).start()

    def z_chip(kind, own_ref, g):
        if kind != S:
            x_copy(kind, g * per, per, g).wait_recv()
        for i in range(per):
            c = g * per + i
            for q in range(cap):
                request = ask(kind, OWN, c, q)
                block = own_ref[jnp.clip(request, 0, hold - 1)]
                if kind != S:
                    block = jnp.where(request < hold, block, xrecvs[kind][c * cap + q])
                if kind == T:
                    block = block.T
                sends[kind][c * cap + q] = block

            @pl.when(c != me)
            def _(c=c):
                z_copy(kind, c).start()

    def keep(kind):
        for q in range(cap):
            fetched[kind][me * cap + q] = sends[kind][me * cap + q]

    def near(j):
        below = lax.div(chip + chips - j, chips)
        return j + below * (chip - 2 * j)

    half = (chips + 1) // 2
    turns = list(range(half)) + list(range(half, chips))[::-1]

    def others_first(j):
        if j == chips - 1:
            return chip
        return j + lax.div(j + chips - chip, chips)

    def z_chips(low, high):
        for j in range(low, high):
            z_chip(Z, z_ref, turns[j])

    def arrived(kind):
        z_all(kind).wait_recv()

    def product(kind, local_ref, finish):
        f = fetched[kind]

        def body(g):
            rhs = local_ref[pl.ds(g * slots, slots)].reshape(slots * size, size)
            for a in range(slots):
                blocks = []
                for b in range(slots):
                    name = pairs[kind][g, a, b]
                    blocks.append(f[jnp.where(name < 0, fetch, name)])
                lhs = jnp.concatenate(blocks, axis=1)
                finish(g * slots + a, a, jnp.dot(lhs, rhs, preferred_element_type=jnp.float32))

        lax.fori_loop(0, cols, lambda g, c: (body(g), c)[1], 0, unroll=True)

    def first(j):
        g = near(j)
        asked(OWN, g)
        z_chip(S, s_ref, g)
        asked(OTHER, g)
        x_chip(T, z_ref, g)

    with jax.named_scope("first"):
        each_chip(0, chips, first)
    with jax.named_scope("xZ"):
        for g in turns:
            x_chip(Z, z_ref, g)
    with jax.named_scope("zT"):
        each_chip(0, chips, lambda j: z_chip(T, z_ref, near(j)))
        keep(S)
        keep(T)

    for load in loads[6:]:
        load.wait()
    with jax.named_scope("arrS"):
        arrived(S)

    def y_finish(i, a, total):
        y_ref[i] = total.astype(y_ref.dtype)

    with jax.named_scope("pY"):
        product(S, z_ref, y_finish)
    with jax.named_scope("zZ1"):
        z_chips(0, half)
    with jax.named_scope("arrT"):
        arrived(T)
        z_chips(half, half + 1)

    def d_finish(i, a, total):
        rows = lax.broadcasted_iota(jnp.int32, (size, size), 0)
        columns = lax.broadcasted_iota(jnp.int32, (size, size), 1)
        one = 1.0 if a == 0 else 0.0
        d_ref[i] = (jnp.where(rows == columns, one, 0.0) - total).astype(d_ref.dtype)

    with jax.named_scope("pD"):
        product(T, y_ref, d_finish)
    with jax.named_scope("xD"):
        for j in range(chips):
            x_chip(D, d_ref, others_first(j))
    with jax.named_scope("zZ2"):
        z_chips(half + 1, chips)
        keep(Z)
    with jax.named_scope("zD"):
        for j in range(chips):
            z_chip(D, d_ref, others_first(j))
        keep(D)
    with jax.named_scope("arrD"):
        arrived(D)

    def e_finish(i, a, total):
        e_ref[i] = (0.5 * d_ref[i].astype(jnp.float32) + 0.375 * total).astype(e_ref.dtype)

    with jax.named_scope("pE"):
        product(D, d_ref, e_finish)
    with jax.named_scope("arrZ"):
        arrived(Z)

    def z_finish(i, a, total):
        out_ref[i] = (z_ref[i].astype(jnp.float32) + total).astype(out_ref.dtype)

    with jax.named_scope("pO"):
        product(Z, e_ref, z_finish)

    for side in (OWN, OTHER):
        rows = allreq.at[pl.ds(0, n - 1 + side)]
        pltpu.make_async_remote_copy(
            src_ref=rows,
            dst_ref=rows,
            send_sem=req_send.at[side],
            recv_sem=req_recv.at[side, 0],
            device_id=(leaf, me),
            device_id_type=MESH,
        ).wait_send()
    for kind in (S, T, Z, D):
        z_all(kind).wait_send()
        if kind != S:
            x_copy(kind, 0, n, 0).wait_send()


def on_device(
    n,
    s_blocks,
    z_blocks,
    s_requests,
    y_pairs,
    zt_requests,
    d_pairs,
    d_requests,
    e_pairs,
    z_requests,
    z_pairs,
):
    cols, slots, size = z_blocks.shape[:3]
    cap = s_requests.shape[3]
    per = 1 + (n + 1) % 2
    hold = cols * slots
    flat = (hold, size, size)
    fetch = n * cap
    asks = [
        r.reshape(1, fetch) for r in (s_requests, zt_requests, z_requests, d_requests)
    ]
    names = [y_pairs, d_pairs, e_pairs, z_pairs]
    kind = z_blocks.dtype

    def blocks(count):
        return pltpu.VMEM((count, size, size), kind)

    hbm = pl.BlockSpec(memory_space=pltpu.HBM)
    refined = pl.pallas_call(
        functools.partial(kernel, n, per, cap, cols, slots),
        out_shape=pltpu.VMEM(flat, kind),
        in_specs=[hbm] * 10,
        out_specs=pl.BlockSpec(memory_space=pltpu.VMEM),
        scratch_shapes=[
            pltpu.VMEM((4, fetch), jnp.int32),
            pltpu.SMEM((2 * n, 4, fetch), jnp.int32),
        ]
        + [pltpu.SMEM(y_pairs.shape, jnp.int32) for _ in range(4)]
        + [blocks(hold) for _ in range(2)]
        + [blocks(fetch) for _ in range(10)]
        + [blocks(fetch + 1) for _ in range(4)]
        + [blocks(hold) for _ in range(3)]
        + [
            pltpu.SemaphoreType.REGULAR((2, n // per)),
            pltpu.SemaphoreType.DMA((2,)),
            pltpu.SemaphoreType.DMA((2, n // per)),
            pltpu.SemaphoreType.DMA((10,)),
            pltpu.SemaphoreType.DMA((4,)),
            pltpu.SemaphoreType.DMA((4,)),
            pltpu.SemaphoreType.DMA((3,)),
            pltpu.SemaphoreType.DMA((3, n // per)),
        ],
        compiler_params=pltpu.CompilerParams(
            collective_id=0, has_side_effects=True, vmem_limit_bytes=66326528
        ),
    )(*asks, *names, s_blocks.reshape(flat), z_blocks.reshape(flat))
    return refined.reshape(z_blocks.shape)


def solution(mesh):
    flat4 = P(("leaf", "col"), None, None, None)
    flat3 = P(("leaf", "col"), None, None)
    asks = P("leaf", "col", None, None)
    in_specs = (flat4, flat4, asks, flat3, asks, flat3, asks, flat3, asks, flat3)
    return jax.shard_map(
        functools.partial(on_device, mesh.shape["col"]),
        mesh=mesh,
        in_specs=in_specs,
        out_specs=flat4,
        check_vma=False,
    )
```

```python
import functools

import jax
import jax.numpy as jnp
from jax import lax
from jax.experimental import pallas as pl
from jax.experimental.pallas import tpu as pltpu
from jax.sharding import PartitionSpec as P

MESH = pl.DeviceIdType.MESH
S, T, Z, D = range(4)
OWN, OTHER = range(2)


def kernel(
    n,
    per,
    cap,
    cols,
    slots,
    s_asks,
    t_asks,
    z_asks,
    d_asks,
    y_names,
    d_names,
    e_names,
    z_names,
    s_hbm,
    z_hbm,
    out_ref,
    req_ref,
    allreq,
    y_pairs,
    d_pairs,
    e_pairs,
    z_pairs,
    s_ref,
    z_ref,
    send_s,
    send_t,
    send_z,
    send_d,
    xs_t,
    xs_z,
    xs_d,
    xr_t,
    xr_z,
    xr_d,
    f_s,
    f_t,
    f_z,
    f_d,
    y_ref,
    d_ref,
    e_ref,
    go_sem,
    req_send,
    req_recv,
    in_sem,
    z_send,
    z_recv,
    x_send,
    x_recv,
    xd_recv,
):
    leaf = lax.axis_index("leaf")
    me = lax.axis_index("col")
    odd = lax.rem(leaf, 2)
    partner = leaf + 1 - 2 * odd
    chips = n // per
    chip = lax.div(me, per)
    hold = cols * slots
    size = z_ref.shape[1]
    fetch = n * cap
    pairs = {S: y_pairs, T: d_pairs, D: e_pairs, Z: z_pairs}
    asks = (s_asks, t_asks, z_asks, d_asks)
    moves = [(a, req_ref.at[pl.ds(kind, 1)]) for kind, a in enumerate(asks)]
    moves += [(s_hbm, s_ref), (z_hbm, z_ref)]
    moves += [(y_names, y_pairs), (d_names, d_pairs), (e_names, e_pairs), (z_names, z_pairs)]
    loads = [pltpu.make_async_copy(a, b, in_sem.at[i]) for i, (a, b) in enumerate(moves)]
    sends = {S: send_s, T: send_t, Z: send_z, D: send_d}
    fetched = {S: f_s, T: f_t, Z: f_z, D: f_d}
    xsends = {T: xs_t, Z: xs_z, D: xs_d}
    xrecvs = {T: xr_t, Z: xr_z, D: xr_d}
    leaves = (leaf, partner)

    def span(low, high, body):
        def step(k, carry):
            body(k)
            return carry

        lax.fori_loop(low, high, step, 0)

    def each_chip(low, high, body):
        def step(k, carry):
            body(k)
            return carry

        lax.fori_loop(low, high, step, 0, unroll=n <= 8)

    barrier = pltpu.get_barrier_semaphore()

    def greet(to_leaf, to):
        pl.semaphore_signal(barrier, inc=1, device_id=(to_leaf, to), device_id_type=MESH)

    def greet_chip(side, c):
        for i in range(per):
            greet(leaves[side], c * per + i)

    def tell_chip(side, c):
        for i in range(per):
            pl.semaphore_signal(
                go_sem.at[side, chip],
                inc=1,
                device_id=(leaves[side], c * per + i),
                device_id_type=MESH,
            )

    for i in range(1, per):
        greet(leaf, chip * per + lax.rem(me + i, per))
    for load in loads:
        load.start()

    @pl.when(odd == 0)
    def _():
        greet_chip(OTHER, chip)

    def greet_up(c):
        greet_chip(OWN, c)
        greet_chip(OTHER, c)

    span(chip + 1, chips, greet_up)
    for f in (f_s, f_t, f_z, f_d):
        f[fetch] = jnp.zeros((size, size), f.dtype)
    pl.semaphore_wait(barrier, per - 1 + per * odd + 2 * per * chip)

    @pl.when(odd == 1)
    def _():
        tell_chip(OTHER, chip)

    def tell_down(k):
        tell_chip(OWN, chip - k)
        tell_chip(OTHER, chip - k)

    span(1, chip + 1, tell_down)
    for load in loads[:4]:
        load.wait()
    own_copy = pltpu.make_async_copy(req_ref, allreq.at[me], req_recv.at[OWN, chip])
    own_copy.start()

    def req_copy(side, to):
        return pltpu.make_async_remote_copy(
            src_ref=req_ref,
            dst_ref=allreq.at[side * n + me],
            send_sem=req_send.at[side],
            recv_sem=req_recv.at[side, chip],
            device_id=(leaves[side], to),
            device_id_type=MESH,
        )

    def ask_chip(side, c):
        for i in range(per):
            req_copy(side, c * per + i).start()

    for i in range(1, per):
        req_copy(OWN, chip * per + lax.rem(me + i, per)).start()

    @pl.when(odd == 1)
    def _():
        ask_chip(OTHER, chip)

    def ask_down(k):
        ask_chip(OWN, chip - k)
        ask_chip(OTHER, chip - k)

    span(1, chip + 1, ask_down)

    @pl.when(odd == 0)
    def _():
        pl.semaphore_wait(go_sem.at[OTHER, chip], per)
        ask_chip(OTHER, chip)

    def ask_up(c):
        for side in (OWN, OTHER):
            pl.semaphore_wait(go_sem.at[side, c], per)
            ask_chip(side, c)

    span(chip + 1, chips, ask_up)
    for load in loads[4:6]:
        load.wait()

    def asked(side, c):
        rows = allreq.at[pl.ds(side * n + c * per, per)]
        pltpu.make_async_remote_copy(
            src_ref=rows,
            dst_ref=rows,
            send_sem=req_send.at[side],
            recv_sem=req_recv.at[side, c],
            device_id=(leaf, me),
            device_id_type=MESH,
        ).wait_recv()

    def ask(kind, side, c, q):
        return allreq[side * n + c, kind, me * cap + q]

    def x_copy(kind, first, count):
        part = pl.ds(first * cap, count * cap)
        landed = xd_recv.at[first] if kind == D else x_recv.at[kind - 1, lax.div(first, per)]
        return pltpu.make_async_remote_copy(
            src_ref=xsends[kind].at[part],
            dst_ref=xrecvs[kind].at[part],
            send_sem=x_send.at[kind - 1],
            recv_sem=landed,
            device_id=(partner, me),
            device_id_type=MESH,
        )

    def z_copy(kind, to):
        return pltpu.make_async_remote_copy(
            src_ref=sends[kind].at[pl.ds(to * cap, cap)],
            dst_ref=fetched[kind].at[pl.ds(me * cap, cap)],
            send_sem=z_send.at[kind],
            recv_sem=z_recv.at[kind],
            device_id=(leaf, to),
            device_id_type=MESH,
        )

    def z_all(kind):
        part = pl.ds(0, (n - 1) * cap)
        return pltpu.make_async_remote_copy(
            src_ref=sends[kind].at[part],
            dst_ref=fetched[kind].at[part],
            send_sem=z_send.at[kind],
            recv_sem=z_recv.at[kind],
            device_id=(leaf, me),
            device_id_type=MESH,
        )

    def x_chip(kind, own_ref, g):
        for i in range(per):
            c = g * per + i
            for q in range(cap):
                slot = jnp.clip(ask(kind, OTHER, c, q) - hold, 0, hold - 1)
                xsends[kind][c * cap + q] = own_ref[slot]
            x_copy(kind, c, 1).start()

    def z_chip(kind, own_ref, g):
        if kind in (T, Z):
            x_copy(kind, g * per, per).wait_recv()
        for i in range(per):
            c = g * per + i
            if kind == D:
                x_copy(kind, c, 1).wait_recv()
            for q in range(cap):
                request = ask(kind, OWN, c, q)
                block = own_ref[jnp.clip(request, 0, hold - 1)]
                if kind != S:
                    block = jnp.where(request < hold, block, xrecvs[kind][c * cap + q])
                if kind == T:
                    block = block.T
                sends[kind][c * cap + q] = block

            @pl.when(c != me)
            def _(c=c):
                z_copy(kind, c).start()

    def keep(kind):
        for q in range(cap):
            fetched[kind][me * cap + q] = sends[kind][me * cap + q]

    def near(j):
        below = lax.div(chip + chips - j, chips)
        return j + below * (chip - 2 * j)

    half = (chips + 1) // 2
    turns = list(range(half)) + list(range(half, chips))[::-1]

    def others_first(j):
        if j == chips - 1:
            return chip
        return j + lax.div(j + chips - chip, chips)

    def z_chips(low, high):
        for j in range(low, high):
            z_chip(Z, z_ref, turns[j])

    def arrived(kind):
        z_all(kind).wait_recv()

    def product(kind, local_ref, finish):
        f = fetched[kind]

        def body(g):
            rhs = local_ref[pl.ds(g * slots, slots)].reshape(slots * size, size)
            for a in range(slots):
                blocks = []
                for b in range(slots):
                    name = pairs[kind][g, a, b]
                    blocks.append(f[jnp.where(name < 0, fetch, name)])
                lhs = jnp.concatenate(blocks, axis=1)
                finish(g * slots + a, a, jnp.dot(lhs, rhs, preferred_element_type=jnp.float32))

        lax.fori_loop(0, cols, lambda g, c: (body(g), c)[1], 0, unroll=True)

    def first(j):
        g = near(j)
        asked(OWN, g)
        z_chip(S, s_ref, g)
        asked(OTHER, g)
        x_chip(T, z_ref, g)

    with jax.named_scope("first"):
        each_chip(0, chips, first)
    with jax.named_scope("xZ"):
        for g in turns:
            x_chip(Z, z_ref, g)
    with jax.named_scope("zT"):
        each_chip(0, chips, lambda j: z_chip(T, z_ref, near(j)))
        keep(S)
        keep(T)

    for load in loads[6:]:
        load.wait()
    with jax.named_scope("arrS"):
        arrived(S)

    def y_finish(i, a, total):
        y_ref[i] = total.astype(y_ref.dtype)

    with jax.named_scope("pY"):
        product(S, z_ref, y_finish)
    with jax.named_scope("zZ1"):
        z_chips(0, half)
    with jax.named_scope("arrT"):
        arrived(T)
        z_chips(half, half + 1)

    def d_finish(i, a, total):
        rows = lax.broadcasted_iota(jnp.int32, (size, size), 0)
        columns = lax.broadcasted_iota(jnp.int32, (size, size), 1)
        one = 1.0 if a == 0 else 0.0
        d_ref[i] = (jnp.where(rows == columns, one, 0.0) - total).astype(d_ref.dtype)

    with jax.named_scope("pD"):
        product(T, y_ref, d_finish)
    with jax.named_scope("xD"):
        for j in range(chips):
            x_chip(D, d_ref, others_first(j))
    with jax.named_scope("zZ2"):
        z_chips(half + 1, chips)
        keep(Z)
    with jax.named_scope("zD"):
        for j in range(chips):
            z_chip(D, d_ref, others_first(j))
        keep(D)
    with jax.named_scope("arrD"):
        arrived(D)

    def e_finish(i, a, total):
        e_ref[i] = (0.5 * d_ref[i].astype(jnp.float32) + 0.375 * total).astype(e_ref.dtype)

    with jax.named_scope("pE"):
        product(D, d_ref, e_finish)
    with jax.named_scope("arrZ"):
        arrived(Z)

    def z_finish(i, a, total):
        out_ref[i] = (z_ref[i].astype(jnp.float32) + total).astype(out_ref.dtype)

    with jax.named_scope("pO"):
        product(Z, e_ref, z_finish)

    for side in (OWN, OTHER):
        rows = allreq.at[pl.ds(0, n - 1 + side)]
        pltpu.make_async_remote_copy(
            src_ref=rows,
            dst_ref=rows,
            send_sem=req_send.at[side],
            recv_sem=req_recv.at[side, 0],
            device_id=(leaf, me),
            device_id_type=MESH,
        ).wait_send()
    for kind in (S, T, Z, D):
        z_all(kind).wait_send()
        if kind != S:
            x_copy(kind, 0, n).wait_send()


def on_device(
    n,
    s_blocks,
    z_blocks,
    s_requests,
    y_pairs,
    zt_requests,
    d_pairs,
    d_requests,
    e_pairs,
    z_requests,
    z_pairs,
):
    cols, slots, size = z_blocks.shape[:3]
    cap = s_requests.shape[3]
    per = 1 + (n + 1) % 2
    hold = cols * slots
    flat = (hold, size, size)
    fetch = n * cap
    asks = [
        r.reshape(1, fetch) for r in (s_requests, zt_requests, z_requests, d_requests)
    ]
    names = [y_pairs, d_pairs, e_pairs, z_pairs]
    kind = z_blocks.dtype

    def blocks(count):
        return pltpu.VMEM((count, size, size), kind)

    hbm = pl.BlockSpec(memory_space=pltpu.HBM)
    refined = pl.pallas_call(
        functools.partial(kernel, n, per, cap, cols, slots),
        out_shape=pltpu.VMEM(flat, kind),
        in_specs=[hbm] * 10,
        out_specs=pl.BlockSpec(memory_space=pltpu.VMEM),
        scratch_shapes=[
            pltpu.VMEM((4, fetch), jnp.int32),
            pltpu.SMEM((2 * n, 4, fetch), jnp.int32),
        ]
        + [pltpu.SMEM(y_pairs.shape, jnp.int32) for _ in range(4)]
        + [blocks(hold) for _ in range(2)]
        + [blocks(fetch) for _ in range(10)]
        + [blocks(fetch + 1) for _ in range(4)]
        + [blocks(hold) for _ in range(3)]
        + [
            pltpu.SemaphoreType.REGULAR((2, n // per)),
            pltpu.SemaphoreType.DMA((2,)),
            pltpu.SemaphoreType.DMA((2, n // per)),
            pltpu.SemaphoreType.DMA((10,)),
            pltpu.SemaphoreType.DMA((4,)),
            pltpu.SemaphoreType.DMA((4,)),
            pltpu.SemaphoreType.DMA((3,)),
            pltpu.SemaphoreType.DMA((2, n // per)),
            pltpu.SemaphoreType.DMA((n,)),
        ],
        compiler_params=pltpu.CompilerParams(
            collective_id=0, has_side_effects=True, vmem_limit_bytes=66326528
        ),
    )(*asks, *names, s_blocks.reshape(flat), z_blocks.reshape(flat))
    return refined.reshape(z_blocks.shape)


def solution(mesh):
    flat4 = P(("leaf", "col"), None, None, None)
    flat3 = P(("leaf", "col"), None, None)
    asks = P("leaf", "col", None, None)
    in_specs = (flat4, flat4, asks, flat3, asks, flat3, asks, flat3, asks, flat3)
    return jax.shard_map(
        functools.partial(on_device, mesh.shape["col"]),
        mesh=mesh,
        in_specs=in_specs,
        out_specs=flat4,
        check_vma=False,
    )
```

```python
import functools

import jax
import jax.numpy as jnp
from jax import lax
from jax.experimental import pallas as pl
from jax.experimental.pallas import tpu as pltpu
from jax.sharding import PartitionSpec as P

MESH = pl.DeviceIdType.MESH
S, T, Z, D = range(4)
OWN, OTHER = range(2)


def kernel(
    n,
    per,
    cap,
    cols,
    slots,
    s_asks,
    t_asks,
    z_asks,
    d_asks,
    y_names,
    d_names,
    e_names,
    z_names,
    s_hbm,
    z_hbm,
    out_ref,
    req_ref,
    allreq,
    y_pairs,
    d_pairs,
    e_pairs,
    z_pairs,
    s_ref,
    z_ref,
    send_s,
    send_t,
    send_z,
    send_d,
    xs_t,
    xs_z,
    xs_d,
    xr_t,
    xr_z,
    xr_d,
    f_s,
    f_t,
    f_z,
    f_d,
    y_ref,
    d_ref,
    e_ref,
    go_sem,
    req_send,
    req_recv,
    in_sem,
    z_send,
    z_recv,
    x_send,
    x_recv,
    xd_recv,
    cross_ref,
    cross_recv,
):
    leaf = lax.axis_index("leaf")
    me = lax.axis_index("col")
    odd = lax.rem(leaf, 2)
    partner = leaf + 1 - 2 * odd
    chips = n // per
    chip = lax.div(me, per)
    hold = cols * slots
    size = z_ref.shape[1]
    fetch = n * cap
    pairs = {S: y_pairs, T: d_pairs, D: e_pairs, Z: z_pairs}
    asks = (s_asks, t_asks, z_asks, d_asks)
    moves = [(a, req_ref.at[pl.ds(kind, 1)]) for kind, a in enumerate(asks)]
    moves += [(s_hbm, s_ref), (z_hbm, z_ref)]
    moves += [(y_names, y_pairs), (d_names, d_pairs), (e_names, e_pairs), (z_names, z_pairs)]
    loads = [pltpu.make_async_copy(a, b, in_sem.at[i]) for i, (a, b) in enumerate(moves)]
    sends = {S: send_s, T: send_t, Z: send_z, D: send_d}
    fetched = {S: f_s, T: f_t, Z: f_z, D: f_d}
    xsends = {T: xs_t, Z: xs_z, D: xs_d}
    xrecvs = {T: xr_t, Z: xr_z, D: xr_d}
    leaves = (leaf, partner)

    def span(low, high, body):
        def step(k, carry):
            body(k)
            return carry

        lax.fori_loop(low, high, step, 0)

    def each_chip(low, high, body):
        def step(k, carry):
            body(k)
            return carry

        lax.fori_loop(low, high, step, 0, unroll=n <= 8)

    barrier = pltpu.get_barrier_semaphore()

    def greet(to_leaf, to):
        pl.semaphore_signal(barrier, inc=1, device_id=(to_leaf, to), device_id_type=MESH)

    def greet_chip(side, c):
        for i in range(per):
            greet(leaves[side], c * per + i)

    def tell_chip(side, c):
        for i in range(per):
            pl.semaphore_signal(
                go_sem.at[side, chip],
                inc=1,
                device_id=(leaves[side], c * per + i),
                device_id_type=MESH,
            )

    for i in range(1, per):
        greet(leaf, chip * per + lax.rem(me + i, per))
    for load in loads:
        load.start()

    @pl.when(odd == 0)
    def _():
        greet_chip(OTHER, chip)

    def greet_up(c):
        greet_chip(OWN, c)
        greet_chip(OTHER, c)

    span(chip + 1, chips, greet_up)
    for f in (f_s, f_t, f_z, f_d):
        f[fetch] = jnp.zeros((size, size), f.dtype)
    pl.semaphore_wait(barrier, per - 1 + per * odd + 2 * per * chip)

    @pl.when(odd == 1)
    def _():
        tell_chip(OTHER, chip)

    def tell_down(k):
        tell_chip(OWN, chip - k)
        tell_chip(OTHER, chip - k)

    span(1, chip + 1, tell_down)
    for load in loads[:4]:
        load.wait()
    own_copy = pltpu.make_async_copy(req_ref, allreq.at[me], req_recv.at[OWN, chip])
    own_copy.start()

    def req_copy(side, to):
        return pltpu.make_async_remote_copy(
            src_ref=req_ref,
            dst_ref=allreq.at[side * n + me],
            send_sem=req_send.at[side],
            recv_sem=req_recv.at[side, chip],
            device_id=(leaves[side], to),
            device_id_type=MESH,
        )

    def ask_chip(side, c):
        for i in range(per):
            req_copy(side, c * per + i).start()

    for i in range(1, per):
        req_copy(OWN, chip * per + lax.rem(me + i, per)).start()

    @pl.when(odd == 1)
    def _():
        ask_chip(OTHER, chip)

    def ask_down(k):
        ask_chip(OWN, chip - k)
        ask_chip(OTHER, chip - k)

    span(1, chip + 1, ask_down)

    @pl.when(odd == 0)
    def _():
        pl.semaphore_wait(go_sem.at[OTHER, chip], per)
        ask_chip(OTHER, chip)

    def ask_up(c):
        for side in (OWN, OTHER):
            pl.semaphore_wait(go_sem.at[side, c], per)
            ask_chip(side, c)

    span(chip + 1, chips, ask_up)
    for load in loads[4:6]:
        load.wait()

    def asked(side, c):
        rows = allreq.at[pl.ds(side * n + c * per, per)]
        pltpu.make_async_remote_copy(
            src_ref=rows,
            dst_ref=rows,
            send_sem=req_send.at[side],
            recv_sem=req_recv.at[side, c],
            device_id=(leaf, me),
            device_id_type=MESH,
        ).wait_recv()

    def ask(kind, side, c, q):
        return allreq[side * n + c, kind, me * cap + q]

    def x_copy(kind, first, count):
        part = pl.ds(first * cap, count * cap)
        landed = xd_recv.at[first] if kind == D else x_recv.at[kind - 1, lax.div(first, per)]
        return pltpu.make_async_remote_copy(
            src_ref=xsends[kind].at[part],
            dst_ref=xrecvs[kind].at[part],
            send_sem=x_send.at[kind - 1],
            recv_sem=landed,
            device_id=(partner, me),
            device_id_type=MESH,
        )

    def z_copy(kind, to):
        return pltpu.make_async_remote_copy(
            src_ref=sends[kind].at[pl.ds(to * cap, cap)],
            dst_ref=fetched[kind].at[pl.ds(me * cap, cap)],
            send_sem=z_send.at[kind],
            recv_sem=z_recv.at[kind],
            device_id=(leaf, to),
            device_id_type=MESH,
        )

    def z_all(kind):
        part = pl.ds(0, (n - 1) * cap)
        return pltpu.make_async_remote_copy(
            src_ref=sends[kind].at[part],
            dst_ref=fetched[kind].at[part],
            send_sem=z_send.at[kind],
            recv_sem=z_recv.at[kind],
            device_id=(leaf, me),
            device_id_type=MESH,
        )

    def x_chip(kind, own_ref, g):
        for i in range(per):
            c = g * per + i
            for q in range(cap):
                slot = jnp.clip(ask(kind, OTHER, c, q) - hold, 0, hold - 1)
                xsends[kind][c * cap + q] = own_ref[slot]
            x_copy(kind, c, 1).start()

    others = [chip * per + lax.rem(me + i, per) for i in range(1, per)]

    def cross_copy(to):
        return pltpu.make_async_remote_copy(
            src_ref=xsends[D].at[pl.ds(to * cap, cap)],
            dst_ref=cross_ref,
            send_sem=x_send.at[D - 1],
            recv_sem=cross_recv,
            device_id=(partner, to),
            device_id_type=MESH,
        )

    def x_own_chip():
        for to in [me, *others]:
            for q in range(cap):
                slot = jnp.clip(ask(D, OTHER, to, q) - hold, 0, hold - 1)
                xsends[D][to * cap + q] = d_ref[slot]
            if to is me:
                x_copy(D, me, 1).start()
            else:
                cross_copy(to).start()

    def z_own_chip():
        for other in others:
            for q in range(cap):
                request = ask(D, OWN, other, q)
                sends[D][other * cap + q] = d_ref[jnp.clip(request, 0, hold - 1)]
            z_copy(D, other).start()

    def settle():
        x_copy(D, me, 1).wait_recv()
        for q in range(cap):
            request = ask(D, OWN, me, q)
            block = d_ref[jnp.clip(request, 0, hold - 1)]
            block = jnp.where(request < hold, block, xrecvs[D][me * cap + q])
            fetched[D][me * cap + q] = block
        for other in others:
            cross_copy(other).wait_recv()
            for q in range(cap):
                at = other * cap + q
                request = allreq[me, D, at]
                block = jnp.where(request < hold, fetched[D][at], cross_ref[q])
                fetched[D][at] = block

    def z_chip(kind, own_ref, g):
        if kind in (T, Z):
            x_copy(kind, g * per, per).wait_recv()
        for i in range(per):
            c = g * per + i
            if kind == D:
                x_copy(kind, c, 1).wait_recv()
            for q in range(cap):
                request = ask(kind, OWN, c, q)
                block = own_ref[jnp.clip(request, 0, hold - 1)]
                if kind != S:
                    block = jnp.where(request < hold, block, xrecvs[kind][c * cap + q])
                if kind == T:
                    block = block.T
                sends[kind][c * cap + q] = block

            @pl.when(c != me)
            def _(c=c):
                z_copy(kind, c).start()

    def keep(kind):
        for q in range(cap):
            fetched[kind][me * cap + q] = sends[kind][me * cap + q]

    def near(j):
        below = lax.div(chip + chips - j, chips)
        return j + below * (chip - 2 * j)

    half = (chips + 1) // 2
    turns = list(range(half)) + list(range(half, chips))[::-1]

    def others_first(j):
        return j + lax.div(j + chips - chip, chips)

    def z_chips(low, high):
        for j in range(low, high):
            z_chip(Z, z_ref, turns[j])

    def arrived(kind):
        z_all(kind).wait_recv()

    def product(kind, local_ref, finish):
        f = fetched[kind]

        def body(g):
            rhs = local_ref[pl.ds(g * slots, slots)].reshape(slots * size, size)
            for a in range(slots):
                blocks = []
                for b in range(slots):
                    name = pairs[kind][g, a, b]
                    blocks.append(f[jnp.where(name < 0, fetch, name)])
                lhs = jnp.concatenate(blocks, axis=1)
                finish(g * slots + a, a, jnp.dot(lhs, rhs, preferred_element_type=jnp.float32))

        lax.fori_loop(0, cols, lambda g, c: (body(g), c)[1], 0, unroll=True)

    def first(j):
        g = near(j)
        asked(OWN, g)
        z_chip(S, s_ref, g)
        asked(OTHER, g)
        x_chip(T, z_ref, g)

    with jax.named_scope("first"):
        each_chip(0, chips, first)
    with jax.named_scope("xZ"):
        for g in turns:
            x_chip(Z, z_ref, g)
    with jax.named_scope("zT"):
        each_chip(0, chips, lambda j: z_chip(T, z_ref, near(j)))
        keep(S)
        keep(T)

    for load in loads[6:]:
        load.wait()
    with jax.named_scope("arrS"):
        arrived(S)

    def y_finish(i, a, total):
        y_ref[i] = total.astype(y_ref.dtype)

    with jax.named_scope("pY"):
        product(S, z_ref, y_finish)
    with jax.named_scope("zZ1"):
        z_chips(0, half)
    with jax.named_scope("arrT"):
        arrived(T)
        z_chips(half, half + 1)

    def d_finish(i, a, total):
        rows = lax.broadcasted_iota(jnp.int32, (size, size), 0)
        columns = lax.broadcasted_iota(jnp.int32, (size, size), 1)
        one = 1.0 if a == 0 else 0.0
        d_ref[i] = (jnp.where(rows == columns, one, 0.0) - total).astype(d_ref.dtype)

    with jax.named_scope("pD"):
        product(T, y_ref, d_finish)
    with jax.named_scope("xD"):
        for j in range(chips - 1):
            x_chip(D, d_ref, others_first(j))
        x_own_chip()
    with jax.named_scope("zZ2"):
        z_chips(half + 1, chips)
        keep(Z)
    with jax.named_scope("zD"):
        z_own_chip()
        for j in range(chips - 1):
            z_chip(D, d_ref, others_first(j))
    with jax.named_scope("arrD"):
        arrived(D)
        settle()

    def e_finish(i, a, total):
        e_ref[i] = (0.5 * d_ref[i].astype(jnp.float32) + 0.375 * total).astype(e_ref.dtype)

    with jax.named_scope("pE"):
        product(D, d_ref, e_finish)
    with jax.named_scope("arrZ"):
        arrived(Z)

    def z_finish(i, a, total):
        out_ref[i] = (z_ref[i].astype(jnp.float32) + total).astype(out_ref.dtype)

    with jax.named_scope("pO"):
        product(Z, e_ref, z_finish)

    for side in (OWN, OTHER):
        rows = allreq.at[pl.ds(0, n - 1 + side)]
        pltpu.make_async_remote_copy(
            src_ref=rows,
            dst_ref=rows,
            send_sem=req_send.at[side],
            recv_sem=req_recv.at[side, 0],
            device_id=(leaf, me),
            device_id_type=MESH,
        ).wait_send()
    for kind in (S, T, Z, D):
        z_all(kind).wait_send()
        if kind != S:
            x_copy(kind, 0, n).wait_send()


def on_device(
    n,
    s_blocks,
    z_blocks,
    s_requests,
    y_pairs,
    zt_requests,
    d_pairs,
    d_requests,
    e_pairs,
    z_requests,
    z_pairs,
):
    cols, slots, size = z_blocks.shape[:3]
    cap = s_requests.shape[3]
    per = 1 + (n + 1) % 2
    hold = cols * slots
    flat = (hold, size, size)
    fetch = n * cap
    asks = [
        r.reshape(1, fetch) for r in (s_requests, zt_requests, z_requests, d_requests)
    ]
    names = [y_pairs, d_pairs, e_pairs, z_pairs]
    kind = z_blocks.dtype

    def blocks(count):
        return pltpu.VMEM((count, size, size), kind)

    hbm = pl.BlockSpec(memory_space=pltpu.HBM)
    refined = pl.pallas_call(
        functools.partial(kernel, n, per, cap, cols, slots),
        out_shape=pltpu.VMEM(flat, kind),
        in_specs=[hbm] * 10,
        out_specs=pl.BlockSpec(memory_space=pltpu.VMEM),
        scratch_shapes=[
            pltpu.VMEM((4, fetch), jnp.int32),
            pltpu.SMEM((2 * n, 4, fetch), jnp.int32),
        ]
        + [pltpu.SMEM(y_pairs.shape, jnp.int32) for _ in range(4)]
        + [blocks(hold) for _ in range(2)]
        + [blocks(fetch) for _ in range(10)]
        + [blocks(fetch + 1) for _ in range(4)]
        + [blocks(hold) for _ in range(3)]
        + [
            pltpu.SemaphoreType.REGULAR((2, n // per)),
            pltpu.SemaphoreType.DMA((2,)),
            pltpu.SemaphoreType.DMA((2, n // per)),
            pltpu.SemaphoreType.DMA((10,)),
            pltpu.SemaphoreType.DMA((4,)),
            pltpu.SemaphoreType.DMA((4,)),
            pltpu.SemaphoreType.DMA((3,)),
            pltpu.SemaphoreType.DMA((2, n // per)),
            pltpu.SemaphoreType.DMA((n,)),
            blocks(cap),
            pltpu.SemaphoreType.DMA,
        ],
        compiler_params=pltpu.CompilerParams(
            collective_id=0, has_side_effects=True, vmem_limit_bytes=66326528
        ),
    )(*asks, *names, s_blocks.reshape(flat), z_blocks.reshape(flat))
    return refined.reshape(z_blocks.shape)


def solution(mesh):
    flat4 = P(("leaf", "col"), None, None, None)
    flat3 = P(("leaf", "col"), None, None)
    asks = P("leaf", "col", None, None)
    in_specs = (flat4, flat4, asks, flat3, asks, flat3, asks, flat3, asks, flat3)
    return jax.shard_map(
        functools.partial(on_device, mesh.shape["col"]),
        mesh=mesh,
        in_specs=in_specs,
        out_specs=flat4,
        check_vma=False,
    )
```

```python
import functools

import jax
import jax.numpy as jnp
from jax import lax
from jax.experimental import pallas as pl
from jax.experimental.pallas import tpu as pltpu
from jax.sharding import PartitionSpec as P

MESH = pl.DeviceIdType.MESH
S, T, Z, D = range(4)
OWN, OTHER = range(2)


def kernel(
    n,
    per,
    cap,
    cols,
    slots,
    s_asks,
    t_asks,
    z_asks,
    d_asks,
    y_names,
    d_names,
    e_names,
    z_names,
    s_hbm,
    z_hbm,
    out_ref,
    req_ref,
    allreq,
    y_pairs,
    d_pairs,
    e_pairs,
    z_pairs,
    s_ref,
    z_ref,
    send_s,
    send_t,
    send_z,
    send_d,
    xs_t,
    xs_z,
    xs_d,
    xr_t,
    xr_z,
    xr_d,
    f_s,
    f_t,
    f_z,
    f_d,
    y_ref,
    d_ref,
    e_ref,
    go_sem,
    req_send,
    req_recv,
    in_sem,
    z_send,
    z_recv,
    x_send,
    x_recv,
    xd_recv,
    cross_ref,
    cross_recv,
):
    leaf = lax.axis_index("leaf")
    me = lax.axis_index("col")
    odd = lax.rem(leaf, 2)
    partner = leaf + 1 - 2 * odd
    chips = n // per
    chip = lax.div(me, per)
    hold = cols * slots
    size = z_ref.shape[1]
    fetch = n * cap
    pairs = {S: y_pairs, T: d_pairs, D: e_pairs, Z: z_pairs}
    asks = (s_asks, t_asks, z_asks, d_asks)
    moves = [(a, req_ref.at[pl.ds(kind, 1)]) for kind, a in enumerate(asks)]
    moves += [(s_hbm, s_ref), (z_hbm, z_ref)]
    moves += [(y_names, y_pairs), (d_names, d_pairs), (e_names, e_pairs), (z_names, z_pairs)]
    loads = [pltpu.make_async_copy(a, b, in_sem.at[i]) for i, (a, b) in enumerate(moves)]
    sends = {S: send_s, T: send_t, Z: send_z, D: send_d}
    fetched = {S: f_s, T: f_t, Z: f_z, D: f_d}
    xsends = {T: xs_t, Z: xs_z, D: xs_d}
    xrecvs = {T: xr_t, Z: xr_z, D: xr_d}
    leaves = (leaf, partner)

    def span(low, high, body):
        def step(k, carry):
            body(k)
            return carry

        lax.fori_loop(low, high, step, 0)

    def each_chip(low, high, body):
        def step(k, carry):
            body(k)
            return carry

        lax.fori_loop(low, high, step, 0, unroll=n <= 8)

    barrier = pltpu.get_barrier_semaphore()

    def greet(to_leaf, to):
        pl.semaphore_signal(barrier, inc=1, device_id=(to_leaf, to), device_id_type=MESH)

    def greet_chip(side, c):
        for i in range(per):
            greet(leaves[side], c * per + i)

    def tell_chip(side, c):
        for i in range(per):
            pl.semaphore_signal(
                go_sem.at[side, chip],
                inc=1,
                device_id=(leaves[side], c * per + i),
                device_id_type=MESH,
            )

    for i in range(1, per):
        greet(leaf, chip * per + lax.rem(me + i, per))

    @pl.when(odd == 0)
    def _():
        greet_chip(OTHER, chip)

    def greet_up(c):
        greet_chip(OWN, c)
        greet_chip(OTHER, c)

    span(chip + 1, chips, greet_up)
    for load in loads:
        load.start()
    for f in (f_s, f_t, f_z, f_d):
        f[fetch] = jnp.zeros((size, size), f.dtype)
    pl.semaphore_wait(barrier, per - 1 + per * odd + 2 * per * chip)

    @pl.when(odd == 1)
    def _():
        tell_chip(OTHER, chip)

    def tell_down(k):
        tell_chip(OWN, chip - k)
        tell_chip(OTHER, chip - k)

    span(1, chip + 1, tell_down)
    for load in loads[:4]:
        load.wait()
    own_copy = pltpu.make_async_copy(req_ref, allreq.at[me], req_recv.at[OWN, chip])
    own_copy.start()

    def req_copy(side, to):
        return pltpu.make_async_remote_copy(
            src_ref=req_ref,
            dst_ref=allreq.at[side * n + me],
            send_sem=req_send.at[side],
            recv_sem=req_recv.at[side, chip],
            device_id=(leaves[side], to),
            device_id_type=MESH,
        )

    def ask_chip(side, c):
        for i in range(per):
            req_copy(side, c * per + i).start()

    for i in range(1, per):
        req_copy(OWN, chip * per + lax.rem(me + i, per)).start()

    @pl.when(odd == 1)
    def _():
        ask_chip(OTHER, chip)

    def ask_down(k):
        ask_chip(OWN, chip - k)
        ask_chip(OTHER, chip - k)

    span(1, chip + 1, ask_down)

    @pl.when(odd == 0)
    def _():
        pl.semaphore_wait(go_sem.at[OTHER, chip], per)
        ask_chip(OTHER, chip)

    def ask_up(c):
        for side in (OWN, OTHER):
            pl.semaphore_wait(go_sem.at[side, c], per)
            ask_chip(side, c)

    span(chip + 1, chips, ask_up)
    for load in loads[4:6]:
        load.wait()

    def asked(side, c):
        rows = allreq.at[pl.ds(side * n + c * per, per)]
        pltpu.make_async_remote_copy(
            src_ref=rows,
            dst_ref=rows,
            send_sem=req_send.at[side],
            recv_sem=req_recv.at[side, c],
            device_id=(leaf, me),
            device_id_type=MESH,
        ).wait_recv()

    def ask(kind, side, c, q):
        return allreq[side * n + c, kind, me * cap + q]

    def x_copy(kind, first, count):
        part = pl.ds(first * cap, count * cap)
        landed = xd_recv.at[first] if kind == D else x_recv.at[kind - 1, lax.div(first, per)]
        return pltpu.make_async_remote_copy(
            src_ref=xsends[kind].at[part],
            dst_ref=xrecvs[kind].at[part],
            send_sem=x_send.at[kind - 1],
            recv_sem=landed,
            device_id=(partner, me),
            device_id_type=MESH,
        )

    def z_copy(kind, to):
        return pltpu.make_async_remote_copy(
            src_ref=sends[kind].at[pl.ds(to * cap, cap)],
            dst_ref=fetched[kind].at[pl.ds(me * cap, cap)],
            send_sem=z_send.at[kind],
            recv_sem=z_recv.at[kind],
            device_id=(leaf, to),
            device_id_type=MESH,
        )

    def z_all(kind):
        part = pl.ds(0, (n - 1) * cap)
        return pltpu.make_async_remote_copy(
            src_ref=sends[kind].at[part],
            dst_ref=fetched[kind].at[part],
            send_sem=z_send.at[kind],
            recv_sem=z_recv.at[kind],
            device_id=(leaf, me),
            device_id_type=MESH,
        )

    def x_chip(kind, own_ref, g):
        for i in range(per):
            c = g * per + i
            for q in range(cap):
                slot = jnp.clip(ask(kind, OTHER, c, q) - hold, 0, hold - 1)
                xsends[kind][c * cap + q] = own_ref[slot]
            x_copy(kind, c, 1).start()

    others = [chip * per + lax.rem(me + i, per) for i in range(1, per)]

    def cross_copy(to):
        return pltpu.make_async_remote_copy(
            src_ref=xsends[D].at[pl.ds(to * cap, cap)],
            dst_ref=cross_ref,
            send_sem=x_send.at[D - 1],
            recv_sem=cross_recv,
            device_id=(partner, to),
            device_id_type=MESH,
        )

    def x_own_chip():
        for to in [me, *others]:
            for q in range(cap):
                slot = jnp.clip(ask(D, OTHER, to, q) - hold, 0, hold - 1)
                xsends[D][to * cap + q] = d_ref[slot]
            if to is me:
                x_copy(D, me, 1).start()
            else:
                cross_copy(to).start()

    def z_own_chip():
        for other in others:
            for q in range(cap):
                request = ask(D, OWN, other, q)
                sends[D][other * cap + q] = d_ref[jnp.clip(request, 0, hold - 1)]
            z_copy(D, other).start()

    def z_chip(kind, own_ref, g):
        if kind in (T, Z):
            x_copy(kind, g * per, per).wait_recv()
        for i in range(per):
            c = g * per + i
            if kind == D:
                x_copy(kind, c, 1).wait_recv()
            for q in range(cap):
                request = ask(kind, OWN, c, q)
                block = own_ref[jnp.clip(request, 0, hold - 1)]
                if kind != S:
                    block = jnp.where(request < hold, block, xrecvs[kind][c * cap + q])
                if kind == T:
                    block = block.T
                sends[kind][c * cap + q] = block

            @pl.when(c != me)
            def _(c=c):
                z_copy(kind, c).start()

    def keep(kind):
        for q in range(cap):
            fetched[kind][me * cap + q] = sends[kind][me * cap + q]

    def near(j):
        below = lax.div(chip + chips - j, chips)
        return j + below * (chip - 2 * j)

    half = (chips + 1) // 2
    turns = list(range(half)) + list(range(half, chips))[::-1]

    def others_first(j):
        return j + lax.div(j + chips - chip, chips)

    def z_chips(low, high):
        for j in range(low, high):
            z_chip(Z, z_ref, turns[j])

    def arrived(kind):
        z_all(kind).wait_recv()

    def settle():
        x_copy(D, me, 1).wait_recv()
        for q in range(cap):
            request = ask(D, OWN, me, q)
            block = d_ref[jnp.clip(request, 0, hold - 1)]
            block = jnp.where(request < hold, block, xrecvs[D][me * cap + q])
            fetched[D][me * cap + q] = block
        for other in others:
            cross_copy(other).wait_recv()
        arrived(D)
        for other in others:
            for q in range(cap):
                at = other * cap + q
                request = allreq[me, D, at]
                block = jnp.where(request < hold, fetched[D][at], cross_ref[q])
                fetched[D][at] = block

    def product(kind, local_ref, finish):
        f = fetched[kind]

        def body(g):
            rhs = local_ref[pl.ds(g * slots, slots)].reshape(slots * size, size)
            for a in range(slots):
                blocks = []
                for b in range(slots):
                    name = pairs[kind][g, a, b]
                    blocks.append(f[jnp.where(name < 0, fetch, name)])
                lhs = jnp.concatenate(blocks, axis=1)
                finish(g * slots + a, a, jnp.dot(lhs, rhs, preferred_element_type=jnp.float32))

        lax.fori_loop(0, cols, lambda g, c: (body(g), c)[1], 0, unroll=True)

    def first(j):
        g = near(j)
        asked(OWN, g)
        z_chip(S, s_ref, g)
        asked(OTHER, g)
        x_chip(T, z_ref, g)

    with jax.named_scope("first"):
        each_chip(0, chips, first)
    with jax.named_scope("xZ"):
        for g in turns:
            x_chip(Z, z_ref, g)
    with jax.named_scope("zT"):
        each_chip(0, chips, lambda j: z_chip(T, z_ref, near(j)))
        keep(S)
        keep(T)

    for load in loads[6:]:
        load.wait()
    with jax.named_scope("arrS"):
        arrived(S)

    def y_finish(i, a, total):
        y_ref[i] = total.astype(y_ref.dtype)

    with jax.named_scope("pY"):
        product(S, z_ref, y_finish)
    with jax.named_scope("zZ1"):
        z_chips(0, half)
    with jax.named_scope("arrT"):
        arrived(T)
        z_chips(half, half + 1)

    def d_finish(i, a, total):
        rows = lax.broadcasted_iota(jnp.int32, (size, size), 0)
        columns = lax.broadcasted_iota(jnp.int32, (size, size), 1)
        one = 1.0 if a == 0 else 0.0
        d_ref[i] = (jnp.where(rows == columns, one, 0.0) - total).astype(d_ref.dtype)

    with jax.named_scope("pD"):
        product(T, y_ref, d_finish)
    with jax.named_scope("xD"):
        for j in range(chips - 1):
            x_chip(D, d_ref, others_first(j))
        x_own_chip()
    with jax.named_scope("zZ2"):
        z_chips(half + 1, chips)
        keep(Z)
    with jax.named_scope("zD"):
        z_own_chip()
        for j in range(chips - 1):
            z_chip(D, d_ref, others_first(j))
    with jax.named_scope("arrD"):
        settle()

    def e_finish(i, a, total):
        e_ref[i] = (0.5 * d_ref[i].astype(jnp.float32) + 0.375 * total).astype(e_ref.dtype)

    with jax.named_scope("pE"):
        product(D, d_ref, e_finish)
    with jax.named_scope("arrZ"):
        arrived(Z)

    def z_finish(i, a, total):
        out_ref[i] = (z_ref[i].astype(jnp.float32) + total).astype(out_ref.dtype)

    with jax.named_scope("pO"):
        product(Z, e_ref, z_finish)

    for side in (OWN, OTHER):
        rows = allreq.at[pl.ds(0, n - 1 + side)]
        pltpu.make_async_remote_copy(
            src_ref=rows,
            dst_ref=rows,
            send_sem=req_send.at[side],
            recv_sem=req_recv.at[side, 0],
            device_id=(leaf, me),
            device_id_type=MESH,
        ).wait_send()
    for kind in (S, T, Z, D):
        z_all(kind).wait_send()
        if kind != S:
            x_copy(kind, 0, n).wait_send()


def on_device(
    n,
    s_blocks,
    z_blocks,
    s_requests,
    y_pairs,
    zt_requests,
    d_pairs,
    d_requests,
    e_pairs,
    z_requests,
    z_pairs,
):
    cols, slots, size = z_blocks.shape[:3]
    cap = s_requests.shape[3]
    per = 1 + (n + 1) % 2
    hold = cols * slots
    flat = (hold, size, size)
    fetch = n * cap
    asks = [
        r.reshape(1, fetch) for r in (s_requests, zt_requests, z_requests, d_requests)
    ]
    names = [y_pairs, d_pairs, e_pairs, z_pairs]
    kind = z_blocks.dtype

    def blocks(count):
        return pltpu.VMEM((count, size, size), kind)

    hbm = pl.BlockSpec(memory_space=pltpu.HBM)
    refined = pl.pallas_call(
        functools.partial(kernel, n, per, cap, cols, slots),
        out_shape=pltpu.VMEM(flat, kind),
        in_specs=[hbm] * 10,
        out_specs=pl.BlockSpec(memory_space=pltpu.VMEM),
        scratch_shapes=[
            pltpu.VMEM((4, fetch), jnp.int32),
            pltpu.SMEM((2 * n, 4, fetch), jnp.int32),
        ]
        + [pltpu.SMEM(y_pairs.shape, jnp.int32) for _ in range(4)]
        + [blocks(hold) for _ in range(2)]
        + [blocks(fetch) for _ in range(10)]
        + [blocks(fetch + 1) for _ in range(4)]
        + [blocks(hold) for _ in range(3)]
        + [
            pltpu.SemaphoreType.REGULAR((2, n // per)),
            pltpu.SemaphoreType.DMA((2,)),
            pltpu.SemaphoreType.DMA((2, n // per)),
            pltpu.SemaphoreType.DMA((10,)),
            pltpu.SemaphoreType.DMA((4,)),
            pltpu.SemaphoreType.DMA((4,)),
            pltpu.SemaphoreType.DMA((3,)),
            pltpu.SemaphoreType.DMA((2, n // per)),
            pltpu.SemaphoreType.DMA((n,)),
            blocks(cap),
            pltpu.SemaphoreType.DMA,
        ],
        compiler_params=pltpu.CompilerParams(
            collective_id=0, has_side_effects=True, vmem_limit_bytes=66326528
        ),
    )(*asks, *names, s_blocks.reshape(flat), z_blocks.reshape(flat))
    return refined.reshape(z_blocks.shape)


def solution(mesh):
    flat4 = P(("leaf", "col"), None, None, None)
    flat3 = P(("leaf", "col"), None, None)
    asks = P("leaf", "col", None, None)
    in_specs = (flat4, flat4, asks, flat3, asks, flat3, asks, flat3, asks, flat3)
    return jax.shard_map(
        functools.partial(on_device, mesh.shape["col"]),
        mesh=mesh,
        in_specs=in_specs,
        out_specs=flat4,
        check_vma=False,
    )
```
